512 devices in a mesh: region: 128 (over z, x, core), tm: 4 (over y).
Axes of the slice: x: 4, y: 4, z: 16, core: 2. Of those that a mesh axis runs over, the one named last changes fastest.
Arguments:
- tensor: bfloat16 [32768, 32, 2, 128], P('region'), may hold values from -6 to 6
- g_occ: bfloat16 [4, 16384, 128], P('tm', 'region'), may hold values from -0.375 to 0.375
- g_virt: bfloat16 [4, 16384, 128], P('tm', 'region'), may hold values from -0.375 to 0.375
- offsets: int32 [128, 2], P('region'), may hold values from -1 to 1, as said below
- pattern: int32 [128, 3], P('region'), may hold values from 0 to 1, as said below
Outputs:
- screened: float32 [4, 32768, 768], P('tm', 'region')
The draws below stay inside these ranges and needn't reach their ends.
Inputs may be any that keep to these rules, and one draw needn't show every extreme that they name: Row r holds 2 distinct offsets in increasing order, and r + offset lies within 0 to 127. `pattern`: row r is (b[r-1], 1, b[r]) for bond bits b with b[-1] = b[127] = 0, so that the kept blocks are symmetric.
All inputs are finite; a program needn't handle non-finite values.
Results may differ from the reference program's by a relative error of at most 0.0039.
Values may be sent and summed in bfloat16 or wider, within the bound.
A program may use at most 64 MiB of HBM per device.

```python
import math
import jax
import jax.numpy as jnp
from jax import lax

MU = 32
NU = 128
LAM = 128
KB = 2
ROWS = 256
NREG = 128
NTIME = 4
ORB = 16384
NAUX = 32768


def draw_offsets(key, part):
    omitted = jax.random.randint(key, (NREG,), 0, 3)
    places = jnp.arange(NREG)
    omitted = jnp.where(places == 0, 0, omitted)
    omitted = jnp.where(places == NREG - 1, 2, omitted)
    first_off = jnp.where(omitted == 0, 1, 0)
    second = jnp.where(omitted == 2, 1, 2)
    return (jnp.stack([first_off, second], 1) - 1).astype(jnp.int32)


def draw_pattern(key, part):
    bond_bits = jax.random.randint(jax.random.fold_in(key, 7), (NREG,), 0, 2)
    places = jnp.arange(NREG)
    bond_bits = jnp.where(places == NREG - 1, 0, bond_bits)
    earlier = jnp.concatenate([jnp.zeros((1,), bond_bits.dtype), bond_bits[:-1]])
    return jnp.stack([earlier, jnp.ones_like(bond_bits), bond_bits], 1).astype(jnp.int32)


def shard_levels(key, shape, split, smallest, top_value):
    level = 1.0
    for axis_at, parts in split:
        draws = jax.random.uniform(jax.random.fold_in(jax.random.fold_in(key, 6), axis_at), (parts,), jnp.float32, smallest / len(split), top_value / len(split))
        level = level * jnp.repeat(jnp.exp(draws), shape[axis_at] // parts).reshape((-1,) + (1,) * (len(shape) - 1 - axis_at))
    return level


def gaussian(stream_key, dims, spread, most, split=(), kind=jnp.bfloat16):
    result = jax.random.normal(stream_key, dims, jnp.float32) * spread
    if len(split) > 0:
        result = shard_levels(stream_key, dims, split, -0.22, 0.18) * result
    return jnp.clip(result, min=-most, max=most).astype(kind)


def setup_inputs(seed: int = 0) -> dict:
    keys = jax.random.split(jax.random.key(seed), 6)
    return {
        "tensor": gaussian(keys[0], (NAUX, MU, KB, NU), 1.0, 6.0, ((0, 128),)),
        "g_occ": gaussian(keys[1], (NTIME, ORB, LAM), (KB * NU) ** -0.5, 0.375, ((0, 4), (1, 128))),
        "g_virt": gaussian(keys[2], (NTIME, ORB, LAM), (KB * NU) ** -0.5, 0.375, ((0, 4), (1, 128))),
        "offsets": draw_offsets(jax.random.fold_in(keys[5], 71), 0),
        "pattern": draw_pattern(jax.random.fold_in(keys[5], 71), 0),
    }


time_points = (0.1, 0.5, 1.5, 4.0)
time_weights = (0.2, 0.6, 1.2, 2.5)
omega_points = (0.2, 0.9, 2.5, 7.0)

def cosine_table():
    points = jnp.array(time_points, jnp.float32)
    weights = jnp.array(time_weights, jnp.float32)
    omegas = jnp.array(omega_points, jnp.float32)
    return weights[None, :] * jnp.cos(omegas[:, None] * points[None, :])

def contract(first_op, second_op):
    return lax.dot_general(first_op, second_op, (((1,), (1,)), ((), ())), preferred_element_type=jnp.float32)

def shifted(stacked):
    padding = jnp.zeros_like(stacked[:1])
    previous = jnp.concatenate([padding, stacked[:-1]], 0)
    following = jnp.concatenate([stacked[1:], padding], 0)
    return (previous, following)

def rotate_all(tensor, green, offsets):
    blocks = green.reshape(NREG, NU, 2 * LAM)
    previous, following = shifted(blocks)
    nearby = jnp.stack([previous, blocks, following], 1)
    picked = jnp.take_along_axis(nearby, (offsets + 1).astype(jnp.int32)[:, :, None, None], axis=1)
    tensor_rows = tensor.reshape(NREG, ROWS * MU, KB * NU)

    def per_region(inputs):
        tensor_slab, chosen = inputs
        product = jnp.dot(tensor_slab, chosen.reshape(KB * NU, 2 * LAM), preferred_element_type=jnp.float32)
        product = product.reshape(ROWS, MU, 2, LAM)
        occupied = product[:, :, 0].reshape(ROWS, MU * LAM).astype(jnp.bfloat16)
        virtual = product[:, :, 1].reshape(ROWS, MU * LAM).astype(jnp.bfloat16)
        return (occupied, virtual)
    return lax.map(per_region, (tensor_rows, picked))

def polarize(occupied, virtual, pattern, prefactor):
    occ_prev, occ_next = shifted(occupied)
    virt_prev, virt_next = shifted(virtual)

    def per_region(region_items):
        own_occ, own_virt, prev_occ, prev_virt, next_occ, next_virt, pattern_row = region_items
        mask_weights = pattern_row.astype(jnp.float32)
        left_block = prefactor * (contract(own_occ, prev_virt) + contract(own_virt, prev_occ)) * mask_weights[0]
        middle = prefactor * (contract(own_occ, own_virt) + contract(own_virt, own_occ))
        right_block = prefactor * (contract(own_occ, next_virt) + contract(own_virt, next_occ)) * mask_weights[2]
        return jnp.concatenate([left_block, middle, right_block], 1)
    return lax.map(per_region, (occupied, virtual, occ_prev, virt_prev, occ_next, virt_next, pattern))

def column_block(matrix, position):
    extent = matrix.shape[0]
    return matrix[:, (position + 1) * extent:(position + 2) * extent]

def combine(center_rows, below_rows, above_rows, mask_weights):
    sources = (below_rows, center_rows, above_rows)
    pieces = []
    for target in (-1, 0, 1):
        summed = column_block(center_rows, target)
        for middle in (-1, 0, 1):
            if abs(target - middle) <= 1:
                summed = summed + jnp.dot(column_block(center_rows, middle), column_block(sources[middle + 1], target - middle), precision=lax.Precision.HIGHEST, preferred_element_type=jnp.float32)
        pieces.append(summed * mask_weights[target + 1])
    return jnp.concatenate(pieces, 1)

def screen(freq_rows, pattern):
    previous, following = shifted(freq_rows)

    def per_region(region_items):
        center_rows, below_rows, above_rows, pattern_row = region_items
        return combine(center_rows, below_rows, above_rows, pattern_row.astype(jnp.float32))
    return lax.map(per_region, (freq_rows, previous, following, pattern))

def reference(tensor, g_occ, g_virt, offsets, pattern):
    prefactor = 1.0 / math.sqrt(2.0 * MU * LAM) / (3.0 * ROWS) ** 0.25
    cos_table = cosine_table()
    per_time = []
    for moment in range(NTIME):
        green = jnp.concatenate([g_occ[moment], g_virt[moment]], 1)
        occupied, virtual = rotate_all(tensor, green, offsets)
        per_time.append(polarize(occupied, virtual, pattern, prefactor))
    results = []
    for freq_index in range(NTIME):
        summed = cos_table[freq_index, 0] * per_time[0]
        for moment in range(1, NTIME):
            summed = summed + cos_table[freq_index, moment] * per_time[moment]
        results.append(screen(summed, pattern))
    return jnp.stack(results, 0).reshape(NTIME, NAUX, 3 * ROWS)
```

```python
import functools
import math

import jax
import jax.numpy as jnp
from jax import lax
from jax.experimental import pallas as pl
from jax.experimental.pallas import tpu as pltpu
from jax.sharding import PartitionSpec as P

MESH = pl.DeviceIdType.MESH
F32 = jnp.float32
BF16 = jnp.bfloat16

time_points = (0.1, 0.5, 1.5, 4.0)
time_weights = (0.2, 0.6, 1.2, 2.5)
omega_points = (0.2, 0.9, 2.5, 7.0)
NT = 4
ROWS = 256
MU = 32
NU = 128
LAM = 128
HALF = MU // 2
QROWS = ROWS // NT
PREFACTOR = 1.0 / math.sqrt(2.0 * MU * LAM) / (3.0 * ROWS) ** 0.25
TABLE = [
    [PREFACTOR * w * math.cos(om * t) for t, w in zip(time_points, time_weights)]
    for om in omega_points
]


def dot(a, b):
    return jnp.dot(a, b, preferred_element_type=F32)


def dot_t(a, b):
    return lax.dot_general(a, b, (((1,), (1,)), ((), ())), preferred_element_type=F32)


def split(x):
    high = x.astype(BF16)
    return high, (x - high.astype(F32)).astype(BF16)


def kernel(n_reg, t_hbm, go_hbm, gv_hbm, off_own, pat, out_ref,
           traw, tt, xr, xt, gb, off_in, off_out, pk, own_sw, mm, nh, nl, ndh, ndl, v,
           acc, pb, ra, rb, db, dn, dfull, ybuf, loc_sem, send_sem, recv_sem):
    r = lax.axis_index("region")
    y = lax.axis_index("tm")
    core = lax.rem(r, 2)
    inner = r + 1 - 2 * core
    outer = lax.rem(r - 1 + 2 * core + n_reg, n_reg)
    far_to = lax.rem(r + 2 - 4 * core + n_reg, n_reg)
    far_from = lax.rem(r - 2 + 4 * core + n_reg, n_reg)
    yp = lax.rem(y + 1, NT)
    yo = lax.rem(y + 2, NT)
    ym = lax.rem(y + 3, NT)

    count = [0]
    started = []

    def remote(src, dst, region, tm):
        i = count[0]
        count[0] += 1
        copy = pltpu.make_async_remote_copy(
            src_ref=src, dst_ref=dst, send_sem=send_sem.at[i], recv_sem=recv_sem.at[i],
            device_id=(region, tm), device_id_type=MESH)
        copy.start()
        started.append(copy)
        return copy

    t_copies = []
    for part in range(4):
        rows = pl.ds(part * (ROWS // 4), ROWS // 4)
        copy = pltpu.make_async_copy(t_hbm.at[rows], traw.at[rows], loc_sem.at[part])
        t_copies.append(copy)
    g_copies = [
        pltpu.make_async_copy(go_hbm.at[0], gb.at[y, 0, 0], loc_sem.at[4]),
        pltpu.make_async_copy(gv_hbm.at[0], gb.at[y, 0, 1], loc_sem.at[5]),
    ]
    for copy in g_copies + t_copies:
        copy.start()

    barrier = pltpu.get_barrier_semaphore()
    for region in (inner, outer, far_to, far_from):
        pl.semaphore_signal(barrier, inc=1, device_id=(region, y), device_id_type=MESH)
    for tm in (yp, ym, yo):
        pl.semaphore_signal(barrier, inc=1, device_id=(r, tm), device_id_type=MESH)
    pl.semaphore_wait(barrier, 7)

    xo = [remote(g.at[0], gb.at[y, 1, i], outer, y) for i, g in enumerate((go_hbm, gv_hbm))]
    xf = [remote(g.at[0], gb.at[y, 2, i], far_to, y) for i, g in enumerate((go_hbm, gv_hbm))]
    y1a_p = [remote(g.at[0], gb.at[y, 0, i], r, yp) for i, g in enumerate((go_hbm, gv_hbm))]
    y1a_m = [remote(g.at[0], gb.at[y, 0, i], r, ym) for i, g in enumerate((go_hbm, gv_hbm))]
    xi = [remote(g.at[0], gb.at[y, 3, i], inner, y) for i, g in enumerate((go_hbm, gv_hbm))]
    offs = [remote(off_own, off_in, inner, y), remote(off_own, off_out, outer, y)]
    my_rows = pl.ds(pl.multiple_of(y * QROWS, QROWS), QROWS)

    def half_rows(half):
        return pl.ds(pl.multiple_of(half * 2 * HALF, 2 * HALF), 2 * HALF)

    xt_out = remote(t_hbm.at[my_rows, half_rows(core)], xr.at[1], outer, y)
    xt_in = remote(t_hbm.at[my_rows, half_rows(1 - core)], xr.at[0], inner, y)

    o_at = lax.broadcasted_iota(jnp.int32, (256, 256), 0)
    i_at = lax.broadcasted_iota(jnp.int32, (256, 256), 1)
    swap = ((lax.shift_right_logical(i_at, 4) == (o_at & 15))
            & ((i_at & 15) == lax.shift_right_logical(o_at, 4)))
    swap = jnp.where(swap, 1.0, 0.0).astype(BF16)

    def regroup(blocks):
        joined = jnp.concatenate([b.reshape(256, 128) for b in blocks], 1)
        moved = dot(swap, joined).astype(BF16)
        return [moved[:, i * 128:(i + 1) * 128] for i in range(len(blocks))]

    def own_rows(first, last):
        def step(p, carry):
            at = pl.ds(pl.multiple_of(p * 16, 16), 16)
            for pair in range(2):
                groups = (2 * pair, 2 * pair + 1)
                moved = regroup([traw[at, g * 16:(g + 1) * 16, :] for g in groups])
                for g, block in zip(groups, moved):
                    for q in range(16):
                        lane = (g * 8 + q // 2) * 256 + (q % 2) * 128
                        tt[at, lane:lane + 128] = block[q * 16:(q + 1) * 16]
            return carry
        lax.fori_loop(first, last, step, 0)

    for copy in g_copies:
        copy.wait()
    t_copies[0].wait()
    own_rows(0, 4)

    for copy in xo + xf:
        copy.wait_recv()
    y1b_p = remote(gb.at[y, pl.ds(1, 2)], gb.at[y, pl.ds(1, 2)], r, yp)
    y1b_m = remote(gb.at[y, pl.ds(1, 2)], gb.at[y, pl.ds(1, 2)], r, ym)
    to_inner = [remote(gb.at[y, 1], gb.at[y, 4], inner, y)]

    for copy in y1a_p + y1a_m:
        copy.wait_recv()
    y2a_p = remote(gb.at[ym, 0, 0], gb.at[ym, 0, 0], r, yp)
    y2a_m = remote(gb.at[yp, 0, 1], gb.at[yp, 0, 1], r, ym)
    to_inner.append(remote(gb.at[ym, 0], gb.at[ym, 3], inner, y))
    to_inner.append(remote(gb.at[yp, 0], gb.at[yp, 3], inner, y))

    t_copies[1].wait()
    own_rows(4, 8)

    for copy in (y1b_p, y1b_m):
        copy.wait_recv()
    y2b_p = remote(gb.at[ym, 1], gb.at[ym, 1], r, yp)
    y2b_m = remote(gb.at[yp, 2], gb.at[yp, 2], r, ym)
    to_inner.append(remote(gb.at[ym, 1], gb.at[ym, 4], inner, y))
    to_inner.append(remote(gb.at[yp, 1], gb.at[yp, 4], inner, y))
    y2a_p.wait_recv()
    y2a_m.wait_recv()
    to_inner.append(remote(gb.at[yo, 0], gb.at[yo, 3], inner, y))

    t_copies[2].wait()
    t_copies[3].wait()
    own_rows(8, 16)

    y2b_p.wait_recv()
    to_inner.append(remote(gb.at[yo, 1], gb.at[yo, 4], inner, y))

    xt_in.wait_recv()
    xt_out.wait_recv()
    for side in range(2):
        for qb in range(QROWS // 16):
            groups = (0, 1)
            moved = regroup([xr[side, qb * 16:(qb + 1) * 16, g * 16:(g + 1) * 16, :] for g in groups])
            for g, block in zip(groups, moved):
                for q in range(16):
                    row = (g * 8 + q // 2) * QROWS + qb * 16
                    lane = (q % 2) * 128
                    xt[side, row:row + 16, lane:lane + 128] = block[q * 16:(q + 1) * 16]

    y2b_m.wait_recv()
    for copy in xi + offs + to_inner:
        copy.wait_recv()

    regions = (
        (off_own, 1 + 2 * core, 0, 3 - 2 * core),
        (off_in, 4 * core, 3, 4 - 4 * core),
        (off_out, 2 - 2 * core, 1, 2 * core),
    )
    for place, (off, before, here, after) in enumerate(regions):
        down = jnp.broadcast_to(off[0:1, 0:1], (128, 128)) == -1
        up = jnp.broadcast_to(off[0:1, 1:2], (128, 128)) == 1

        def choose(j, carry, place=place, before=before, here=here, after=after, down=down, up=up):
            for half in range(2):
                mid = gb[j, here, half].astype(F32)
                for slot, (mask, other) in enumerate(((down, before), (up, after))):
                    got = jnp.where(mask, gb[j, other, half].astype(F32), mid).astype(BF16)
                    at = slice(slot * 128, slot * 128 + 128)
                    pk[place, j, at, half * 128:half * 128 + 128] = got
                    if place == 0:
                        own_sw[j, at, (1 - half) * 128:(1 - half) * 128 + 128] = got
            return carry
        lax.fori_loop(0, NT, choose, 0)

    def moments(place):
        def step(j, carry):
            mm[j] = dot_t(pk[place, j], own_sw[j])
            return carry
        lax.fori_loop(0, NT, step, 0)

    for side in range(2):
        moments(1 + side)

        def mix(c, carry):
            at = pl.ds(pl.multiple_of(c * 32, 32), 32)
            terms = [mm[j, at, :] for j in range(NT)]
            for k in range(NT):
                total = TABLE[k][0] * terms[0]
                for j in range(1, NT):
                    total = total + TABLE[k][j] * terms[j]
                high, low = split(total)
                nh[at, k * 256:(k + 1) * 256] = high
                nl[at, k * 256:(k + 1) * 256] = low
            return carry
        lax.fori_loop(0, 8, mix, 0)

        def expand(g, carry, side=side):
            x = xt[side, pl.ds(pl.multiple_of(g * 256, 256), 256), :]
            for k in range(NT):
                cols = slice(k * 256, (k + 1) * 256)
                got = (dot(x, nh[:, cols]) + dot(x, nl[:, cols])).astype(BF16)
                for m in range(4):
                    lane = pl.ds(pl.multiple_of((g * 4 + m) * 256, 256), 256)
                    v[k * QROWS:(k + 1) * QROWS, lane] = got[m * QROWS:(m + 1) * QROWS]
            return carry
        lax.fori_loop(0, 4, expand, 0)

        first = (core if side == 0 else 1 - core) * (HALF * 256)
        acc[...] = jnp.zeros_like(acc)

        def gather(g, carry, first=first):
            left = v[:, pl.ds(pl.multiple_of(g * 1024, 1024), 1024)]
            right = tt[:, pl.ds(pl.multiple_of(first + g * 1024, 1024), 1024)]
            acc[...] += dot_t(left, right)
            return carry
        lax.fori_loop(0, 4, gather, 0)
        for k in range(NT):
            pb[k, side] = acc[k * QROWS:(k + 1) * QROWS].astype(BF16)

    a2a = [remote(pb.at[t], ra.at[y], r, t) for t in (yp, ym, yo)]
    ra[y] = pb[y]
    ex = [remote(pb.at[y, 0], rb.at[0, y], inner, y), remote(pb.at[y, 1], rb.at[1, y], outer, y)]

    moments(0)
    weights = []
    for j in range(NT):
        w = jnp.float32(0.0)
        for k in range(NT):
            w = jnp.where(y == k, jnp.float32(TABLE[k][j]), w)
        weights.append(w)

    def mix_own(c, carry):
        at = pl.ds(pl.multiple_of(c * 32, 32), 32)
        total = weights[0] * mm[0, at, :]
        for j in range(1, NT):
            total = total + weights[j] * mm[j, at, :]
        high, low = split(total)
        ndh[at, :] = high
        ndl[at, :] = low
        return carry
    lax.fori_loop(0, 8, mix_own, 0)
    dfull[...] = jnp.zeros_like(dfull)

    def own_block(g, carry):
        for m in range(4):
            x = tt[:, pl.ds(pl.multiple_of((g * 4 + m) * 256, 256), 256)]
            ybuf[:, m * 256:(m + 1) * 256] = (dot(x, ndh[...]) + dot(x, ndl[...])).astype(BF16)
        dfull[...] += dot_t(ybuf[...], tt[:, pl.ds(pl.multiple_of(g * 1024, 1024), 1024)])
        return carry
    lax.fori_loop(0, MU // 4, own_block, 0)
    db[...] = dfull[...].astype(BF16)
    dx = [remote(db, dn.at[0], inner, y), remote(db, dn.at[1], outer, y)]

    for copy, t in zip(a2a, (ym, yp, yo)):
        copy.wait_recv()
        ex.append(remote(ra.at[t, 0], rb.at[0, t], inner, y))
        ex.append(remote(ra.at[t, 1], rb.at[1, t], outer, y))

    d_high, d_low = split(dfull[...])
    diag = dfull[...] + dot(d_high, d_high) + dot(d_high, d_low) + dot(d_low, d_high)
    for copy in dx + ex:
        copy.wait_recv()
    for side in range(2):
        place = (2 - 2 * core) if side == 0 else 2 * core
        keep = pat[0, place].astype(F32)
        mine = ra[:, side].reshape(ROWS, ROWS).astype(F32)
        block = keep * (rb[side].reshape(ROWS, ROWS).astype(F32) + mine.T)
        high, low = split(block)
        diag = diag + dot_t(high, high) + dot_t(high, low) + dot_t(low, high)
        result = (block + dot(d_high, high) + dot(d_high, low) + dot(d_low, high)
                  + dot(high, dn[side]) + dot(low, dn[side]))
        out_ref[0, :, pl.ds(pl.multiple_of(place * ROWS, ROWS), ROWS)] = keep * result
    out_ref[0, :, ROWS:2 * ROWS] = pat[0, 1].astype(F32) * diag

    for copy in started:
        copy.wait_send()


COPIES = 48


def local(n_reg, tensor, g_occ, g_virt, offsets, pattern):
    anyspace = pl.BlockSpec(memory_space=pl.ANY)
    vmem = pl.BlockSpec(memory_space=pltpu.VMEM)
    return pl.pallas_call(
        functools.partial(kernel, n_reg),
        out_shape=jax.ShapeDtypeStruct((1, ROWS, 3 * ROWS), F32),
        in_specs=[anyspace, anyspace, anyspace, vmem, pl.BlockSpec(memory_space=pltpu.SMEM)],
        out_specs=vmem,
        scratch_shapes=[
            pltpu.VMEM((ROWS, 2 * MU, NU), BF16),
            pltpu.VMEM((ROWS, MU * 256), BF16),
            pltpu.VMEM((2, QROWS, 2 * HALF, NU), BF16),
            pltpu.VMEM((2, HALF * QROWS, 256), BF16),
            pltpu.VMEM((NT, 5, 2, NU, LAM), BF16),
            pltpu.VMEM((1, 2), jnp.int32),
            pltpu.VMEM((1, 2), jnp.int32),
            pltpu.VMEM((3, NT, 256, 256), BF16),
            pltpu.VMEM((NT, 256, 256), BF16),
            pltpu.VMEM((NT, 256, 256), F32),
            pltpu.VMEM((256, NT * 256), BF16),
            pltpu.VMEM((256, NT * 256), BF16),
            pltpu.VMEM((256, 256), BF16),
            pltpu.VMEM((256, 256), BF16),
            pltpu.VMEM((NT * QROWS, HALF * 256), BF16),
            pltpu.VMEM((256, 256), F32),
            pltpu.VMEM((NT, 2, QROWS, 256), BF16),
            pltpu.VMEM((NT, 2, QROWS, 256), BF16),
            pltpu.VMEM((2, NT, QROWS, 256), BF16),
            pltpu.VMEM((256, 256), BF16),
            pltpu.VMEM((2, 256, 256), BF16),
            pltpu.VMEM((256, 256), F32),
            pltpu.VMEM((256, 1024), BF16),
            pltpu.SemaphoreType.DMA((6,)),
            pltpu.SemaphoreType.DMA((COPIES,)),
            pltpu.SemaphoreType.DMA((COPIES,)),
        ],
        compiler_params=pltpu.CompilerParams(collective_id=0, has_side_effects=True),
        name="screen",
    )(tensor.reshape(ROWS, 2 * MU, NU), g_occ, g_virt, offsets, pattern)


def solution(mesh):
    return jax.shard_map(
        functools.partial(local, mesh.shape["region"]),
        mesh=mesh,
        in_specs=(
            P("region", None, None, None),
            P("tm", "region", None),
            P("tm", "region", None),
            P("region", None),
            P("region", None),
        ),
        out_specs=P("tm", "region", None),
        check_vma=False,
    )
```

```python
import functools
import math

import jax
import jax.numpy as jnp
from jax import lax
from jax.experimental import pallas as pl
from jax.experimental.pallas import tpu as pltpu
from jax.sharding import PartitionSpec as P

MESH = pl.DeviceIdType.MESH
F32 = jnp.float32
BF16 = jnp.bfloat16

time_points = (0.1, 0.5, 1.5, 4.0)
time_weights = (0.2, 0.6, 1.2, 2.5)
omega_points = (0.2, 0.9, 2.5, 7.0)
NT = 4
ROWS = 256
MU = 32
NU = 128
LAM = 128
HALF = MU // 2
QROWS = ROWS // NT
PREFACTOR = 1.0 / math.sqrt(2.0 * MU * LAM) / (3.0 * ROWS) ** 0.25
TABLE = [
    [PREFACTOR * w * math.cos(om * t) for t, w in zip(time_points, time_weights)]
    for om in omega_points
]


def dot(a, b):
    return jnp.dot(a, b, preferred_element_type=F32)


def dot_t(a, b):
    return lax.dot_general(a, b, (((1,), (1,)), ((), ())), preferred_element_type=F32)


def split(x):
    high = x.astype(BF16)
    return high, (x - high.astype(F32)).astype(BF16)


def kernel(n_reg, t_hbm, go_hbm, gv_hbm, off_own, pat, out_ref,
           traw, tt, xr, xt, gb, off_in, off_out, pk, own_sw, mm, part, nh, nd, v,
           acc, pb, ra, rb, turned, db, dn, dfull, ybuf, loc_sem, send_sem, recv_sem):
    r = lax.axis_index("region")
    y = lax.axis_index("tm")
    core = lax.rem(r, 2)
    inner = r + 1 - 2 * core
    outer = lax.rem(r - 1 + 2 * core + n_reg, n_reg)
    far_to = lax.rem(r + 2 - 4 * core + n_reg, n_reg)
    far_from = lax.rem(r - 2 + 4 * core + n_reg, n_reg)
    yp = lax.rem(y + 1, NT)
    yo = lax.rem(y + 2, NT)
    ym = lax.rem(y + 3, NT)

    count = [0]
    started = []

    def remote(src, dst, region, tm):
        i = count[0]
        count[0] += 1
        copy = pltpu.make_async_remote_copy(
            src_ref=src, dst_ref=dst, send_sem=send_sem.at[i], recv_sem=recv_sem.at[i],
            device_id=(region, tm), device_id_type=MESH)
        copy.start()
        started.append(copy)
        return copy

    t_copies = []
    for piece in range(4):
        rows = pl.ds(piece * (ROWS // 4), ROWS // 4)
        copy = pltpu.make_async_copy(t_hbm.at[rows], traw.at[rows], loc_sem.at[piece])
        t_copies.append(copy)
    g_copies = [
        pltpu.make_async_copy(go_hbm.at[0], gb.at[y, 0, 0], loc_sem.at[4]),
        pltpu.make_async_copy(gv_hbm.at[0], gb.at[y, 0, 1], loc_sem.at[5]),
    ]
    for copy in g_copies + t_copies:
        copy.start()

    barrier = pltpu.get_barrier_semaphore()
    for region in (inner, outer, far_to, far_from):
        pl.semaphore_signal(barrier, inc=1, device_id=(region, y), device_id_type=MESH)
    for tm in (yp, ym, yo):
        pl.semaphore_signal(barrier, inc=1, device_id=(r, tm), device_id_type=MESH)
    pl.semaphore_wait(barrier, 7)

    xo = [remote(g.at[0], gb.at[y, 1, i], outer, y) for i, g in enumerate((go_hbm, gv_hbm))]
    xf = [remote(g.at[0], gb.at[y, 2, i], far_to, y) for i, g in enumerate((go_hbm, gv_hbm))]
    y1a_p = [remote(g.at[0], gb.at[y, 0, i], r, yp) for i, g in enumerate((go_hbm, gv_hbm))]
    y1a_m = [remote(g.at[0], gb.at[y, 0, i], r, ym) for i, g in enumerate((go_hbm, gv_hbm))]
    xi = [remote(g.at[0], gb.at[y, 3, i], inner, y) for i, g in enumerate((go_hbm, gv_hbm))]
    offs = [remote(off_own, off_in, inner, y), remote(off_own, off_out, outer, y)]
    my_rows = pl.ds(pl.multiple_of(y * QROWS, QROWS), QROWS)

    def half_rows(half):
        return pl.ds(pl.multiple_of(half * 2 * HALF, 2 * HALF), 2 * HALF)

    xt_out = remote(t_hbm.at[my_rows, half_rows(core)], xr.at[1], outer, y)
    xt_in = remote(t_hbm.at[my_rows, half_rows(1 - core)], xr.at[0], inner, y)

    o_at = lax.broadcasted_iota(jnp.int32, (256, 256), 0)
    i_at = lax.broadcasted_iota(jnp.int32, (256, 256), 1)
    swap = ((lax.shift_right_logical(i_at, 4) == (o_at & 15))
            & ((i_at & 15) == lax.shift_right_logical(o_at, 4)))
    swap = jnp.where(swap, 1.0, 0.0).astype(BF16)

    def regroup(blocks):
        joined = jnp.concatenate([b.reshape(256, 128) for b in blocks], 1)
        moved = dot(swap, joined).astype(BF16)
        return [moved[:, i * 128:(i + 1) * 128] for i in range(len(blocks))]

    def own_rows(first, last):
        def step(p, carry):
            at = pl.ds(pl.multiple_of(p * 16, 16), 16)
            for pair in range(2):
                groups = (2 * pair, 2 * pair + 1)
                moved = regroup([traw[at, g * 16:(g + 1) * 16, :] for g in groups])
                for g, block in zip(groups, moved):
                    for q in range(16):
                        lane = (g * 8 + q // 2) * 256 + (q % 2) * 128
                        tt[at, lane:lane + 128] = block[q * 16:(q + 1) * 16]
            return carry
        lax.fori_loop(first, last, step, 0)

    def neighbour_rows():
        for side in range(2):
            for qb in range(QROWS // 16):
                moved = regroup([xr[side, qb * 16:(qb + 1) * 16, g * 16:(g + 1) * 16, :] for g in range(2)])
                for g, block in enumerate(moved):
                    for q in range(16):
                        row = (g * 8 + q // 2) * QROWS + qb * 16
                        lane = (q % 2) * 128
                        xt[side, row:row + 16, lane:lane + 128] = block[q * 16:(q + 1) * 16]

    places = (
        (off_own, 1 + 2 * core, 0, 3 - 2 * core),
        (off_in, 4 * core, 3, 4 - 4 * core),
        (off_out, 2 - 2 * core, 1, 2 * core),
    )

    def moments(j, place):
        off, before, here, after = places[place]
        down = jnp.broadcast_to(off[0:1, 0:1], (128, 128)) == -1
        up = jnp.broadcast_to(off[0:1, 1:2], (128, 128)) == 1
        for half in range(2):
            mid = gb[j, here, half].astype(F32)
            for slot, (mask, other) in enumerate(((down, before), (up, after))):
                got = jnp.where(mask, gb[j, other, half].astype(F32), mid).astype(BF16)
                at = slice(slot * 128, slot * 128 + 128)
                pk[place, at, half * 128:half * 128 + 128] = got
                if place == 0:
                    own_sw[j, at, (1 - half) * 128:(1 - half) * 128 + 128] = got
        mm[place, j] = dot_t(pk[place], own_sw[j])

    def pick_time(column, j):
        w = jnp.float32(column[0])
        for k in range(1, NT):
            w = jnp.where(j == k, jnp.float32(column[k]), w)
        return w

    early = (y, ym, yp)

    def mix_early():
        rows_of_table = [[pick_time(TABLE[k], j) for j in early] for k in range(NT)]

        def step(c, carry):
            at = pl.ds(pl.multiple_of(c * 32, 32), 32)
            for place in (1, 2):
                terms = [mm[place, j, at, :] for j in early]
                for k in range(NT):
                    w = rows_of_table[k]
                    part[place - 1, k, at, :] = w[0] * terms[0] + w[1] * terms[1] + w[2] * terms[2]
            return carry
        lax.fori_loop(0, 8, step, 0)

    def mix_last(place):
        w = [pick_time(TABLE[k], yo) for k in range(NT)]

        def step(c, carry):
            at = pl.ds(pl.multiple_of(c * 32, 32), 32)
            last = mm[place, yo, at, :]
            for k in range(NT):
                nh[at, k * 256:(k + 1) * 256] = (part[place - 1, k, at, :] + w[k] * last).astype(BF16)
            return carry
        lax.fori_loop(0, 8, step, 0)

    for copy in g_copies:
        copy.wait()
    t_copies[0].wait()
    t_copies[1].wait()
    own_rows(0, 8)

    for copy in xo + xf:
        copy.wait_recv()
    y1b_p = remote(gb.at[y, pl.ds(1, 2)], gb.at[y, pl.ds(1, 2)], r, yp)
    y1b_m = remote(gb.at[y, pl.ds(1, 2)], gb.at[y, pl.ds(1, 2)], r, ym)
    in_y = remote(gb.at[y, 1], gb.at[y, 4], inner, y)

    for copy in y1a_p + y1a_m:
        copy.wait_recv()
    y2a_p = remote(gb.at[ym, 0, 0], gb.at[ym, 0, 0], r, yp)
    y2a_m = remote(gb.at[yp, 0, 1], gb.at[yp, 0, 1], r, ym)
    in_m = [remote(gb.at[ym, 0], gb.at[ym, 3], inner, y)]
    in_p = [remote(gb.at[yp, 0], gb.at[yp, 3], inner, y)]

    t_copies[2].wait()
    t_copies[3].wait()
    own_rows(8, 12)

    for copy in (y1b_p, y1b_m):
        copy.wait_recv()
    y2b_p = remote(gb.at[ym, 1], gb.at[ym, 1], r, yp)
    y2b_m = remote(gb.at[yp, 2], gb.at[yp, 2], r, ym)
    in_m.append(remote(gb.at[ym, 1], gb.at[ym, 4], inner, y))
    in_p.append(remote(gb.at[yp, 1], gb.at[yp, 4], inner, y))
    y2a_p.wait_recv()
    y2a_m.wait_recv()
    in_o = [remote(gb.at[yo, 0], gb.at[yo, 3], inner, y)]

    for copy in xi + offs + [in_y]:
        copy.wait_recv()
    for place in range(3):
        moments(y, place)

    own_rows(12, 16)
    y2b_p.wait_recv()
    in_o.append(remote(gb.at[yo, 1], gb.at[yo, 4], inner, y))

    for copy in in_m + in_p:
        copy.wait_recv()
    for place in range(3):
        moments(ym, place)
        moments(yp, place)
    mix_early()
    xt_in.wait_recv()
    xt_out.wait_recv()
    neighbour_rows()

    y2b_m.wait_recv()
    for copy in in_o:
        copy.wait_recv()

    moments(yo, 0)
    a2a, ex = {}, {}
    for side in (1, 0):
        moments(yo, 1 + side)
        mix_last(1 + side)

        def expand(g, carry, side=side):
            x = xt[side, pl.ds(pl.multiple_of(g * 256, 256), 256), :]
            for k in range(NT):
                got = dot(x, nh[:, k * 256:(k + 1) * 256]).astype(BF16)
                for m in range(4):
                    lane = pl.ds(pl.multiple_of((g * 4 + m) * 256, 256), 256)
                    v[k * QROWS:(k + 1) * QROWS, lane] = got[m * QROWS:(m + 1) * QROWS]
            return carry
        lax.fori_loop(0, 4, expand, 0)

        first = (core if side == 0 else 1 - core) * (HALF * 256)
        acc[...] = jnp.zeros_like(acc)

        def gather(g, carry, first=first):
            left = v[:, pl.ds(pl.multiple_of(g * 1024, 1024), 1024)]
            right = tt[:, pl.ds(pl.multiple_of(first + g * 1024, 1024), 1024)]
            acc[...] += dot_t(left, right)
            return carry
        lax.fori_loop(0, 4, gather, 0)
        for k in range(NT):
            pb[k, side] = acc[k * QROWS:(k + 1) * QROWS].astype(BF16)
        a2a[side] = [remote(pb.at[t, side], ra.at[y, side], r, t) for t in (yp, ym, yo)]
        ex[side] = [remote(pb.at[y, side], rb.at[side, y], (inner, outer)[side], y)]
        ra[y, side] = pb[y, side]

    weights = [pick_time([TABLE[k][j] for k in range(NT)], y) for j in range(NT)]

    def mix_own(c, carry):
        at = pl.ds(pl.multiple_of(c * 32, 32), 32)
        total = weights[0] * mm[0, 0, at, :]
        for j in range(1, NT):
            total = total + weights[j] * mm[0, j, at, :]
        nd[at, :] = total.astype(BF16)
        return carry
    lax.fori_loop(0, 8, mix_own, 0)
    dfull[...] = jnp.zeros_like(dfull)

    def own_block(g, carry):
        for m in range(4):
            x = tt[:, pl.ds(pl.multiple_of((g * 4 + m) * 256, 256), 256)]
            ybuf[:, m * 256:(m + 1) * 256] = dot(x, nd[...]).astype(BF16)
        dfull[...] += dot_t(ybuf[...], tt[:, pl.ds(pl.multiple_of(g * 1024, 1024), 1024)])
        return carry
    lax.fori_loop(0, MU // 4, own_block, 0)
    dfull[...] = 0.5 * (dfull[...] + dfull[...].T)
    db[...] = dfull[...].astype(BF16)
    dx = [remote(db, dn.at[0], inner, y), remote(db, dn.at[1], outer, y)]

    for side in (1, 0):
        for copy, t in zip(a2a[side], (ym, yp, yo)):
            copy.wait_recv()
            ex[side].append(remote(ra.at[t, side], rb.at[side, t], (inner, outer)[side], y))
    for side in range(2):
        turned[side] = ra[:, side].reshape(ROWS, ROWS).astype(F32).T

    d_high, d_low = split(dfull[...])
    diag = dfull[...] + dot(d_high, d_high) + dot(d_high, d_low) + dot(d_low, d_high)
    for side in (0, 1):
        dx[side].wait_recv()
        for copy in ex[side]:
            copy.wait_recv()
        place = (2 - 2 * core) if side == 0 else 2 * core
        keep = pat[0, place].astype(F32)
        block = keep * (rb[side].reshape(ROWS, ROWS).astype(F32) + turned[side])
        high, low = split(block)
        diag = diag + dot_t(high, high) + dot_t(high, low) + dot_t(low, high)
        result = (block + dot(d_high, high) + dot(d_high, low) + dot(d_low, high)
                  + dot(high, dn[side]) + dot(low, dn[side]))
        out_ref[0, :, pl.ds(pl.multiple_of(place * ROWS, ROWS), ROWS)] = keep * result
    out_ref[0, :, ROWS:2 * ROWS] = pat[0, 1].astype(F32) * diag

    for copy in started:
        copy.wait_send()


COPIES = 48


def local(n_reg, tensor, g_occ, g_virt, offsets, pattern):
    anyspace = pl.BlockSpec(memory_space=pl.ANY)
    vmem = pl.BlockSpec(memory_space=pltpu.VMEM)
    return pl.pallas_call(
        functools.partial(kernel, n_reg),
        out_shape=pltpu.VMEM((1, ROWS, 3 * ROWS), F32),
        in_specs=[anyspace, anyspace, anyspace, vmem, pl.BlockSpec(memory_space=pltpu.SMEM)],
        out_specs=vmem,
        scratch_shapes=[
            pltpu.VMEM((ROWS, 2 * MU, NU), BF16),
            pltpu.VMEM((ROWS, MU * 256), BF16),
            pltpu.VMEM((2, QROWS, 2 * HALF, NU), BF16),
            pltpu.VMEM((2, HALF * QROWS, 256), BF16),
            pltpu.VMEM((NT, 5, 2, NU, LAM), BF16),
            pltpu.VMEM((1, 2), jnp.int32),
            pltpu.VMEM((1, 2), jnp.int32),
            pltpu.VMEM((3, 256, 256), BF16),
            pltpu.VMEM((NT, 256, 256), BF16),
            pltpu.VMEM((3, NT, 256, 256), F32),
            pltpu.VMEM((2, NT, 256, 256), F32),
            pltpu.VMEM((256, NT * 256), BF16),
            pltpu.VMEM((256, 256), BF16),
            pltpu.VMEM((NT * QROWS, HALF * 256), BF16),
            pltpu.VMEM((256, 256), F32),
            pltpu.VMEM((NT, 2, QROWS, 256), BF16),
            pltpu.VMEM((NT, 2, QROWS, 256), BF16),
            pltpu.VMEM((2, NT, QROWS, 256), BF16),
            pltpu.VMEM((2, ROWS, ROWS), F32),
            pltpu.VMEM((256, 256), BF16),
            pltpu.VMEM((2, 256, 256), BF16),
            pltpu.VMEM((256, 256), F32),
            pltpu.VMEM((256, 1024), BF16),
            pltpu.SemaphoreType.DMA((6,)),
            pltpu.SemaphoreType.DMA((COPIES,)),
            pltpu.SemaphoreType.DMA((COPIES,)),
        ],
        compiler_params=pltpu.CompilerParams(collective_id=0, has_side_effects=True),
        name="screen",
    )(tensor.reshape(ROWS, 2 * MU, NU), g_occ, g_virt, offsets, pattern)


def solution(mesh):
    return jax.shard_map(
        functools.partial(local, mesh.shape["region"]),
        mesh=mesh,
        in_specs=(
            P("region", None, None, None),
            P("tm", "region", None),
            P("tm", "region", None),
            P("region", None),
            P("region", None),
        ),
        out_specs=P("tm", "region", None),
        check_vma=False,
    )
```

```python
import functools
import math

import jax
import jax.numpy as jnp
from jax import lax
from jax.experimental import pallas as pl
from jax.experimental.pallas import tpu as pltpu
from jax.sharding import PartitionSpec as P

MESH = pl.DeviceIdType.MESH
F32 = jnp.float32
BF16 = jnp.bfloat16

time_points = (0.1, 0.5, 1.5, 4.0)
time_weights = (0.2, 0.6, 1.2, 2.5)
omega_points = (0.2, 0.9, 2.5, 7.0)
NT = 4
ROWS = 256
MU = 32
NU = 128
LAM = 128
HALF = MU // 2
QROWS = ROWS // NT
PREFACTOR = 1.0 / math.sqrt(2.0 * MU * LAM) / (3.0 * ROWS) ** 0.25
TABLE = [
    [PREFACTOR * w * math.cos(om * t) for t, w in zip(time_points, time_weights)]
    for om in omega_points
]


def dot(a, b):
    return jnp.dot(a, b, preferred_element_type=F32)


def dot_t(a, b):
    return lax.dot_general(a, b, (((1,), (1,)), ((), ())), preferred_element_type=F32)


def split(x):
    high = x.astype(BF16)
    return high, (x - high.astype(F32)).astype(BF16)


def kernel(n_reg, t_hbm, go_hbm, gv_hbm, off_own, pat, out_ref,
           traw, tt, tin, xr, xt, gb, off_in, off_out, pk, own_sw, mm, part, nh, nd, v,
           acc, pb, ra, rb, pin, rin, turned, db, dn, dfull, ya, yb, loc_sem, send_sem, recv_sem):
    r = lax.axis_index("region")
    y = lax.axis_index("tm")
    core = lax.rem(r, 2)
    inner = r + 1 - 2 * core
    outer = lax.rem(r - 1 + 2 * core + n_reg, n_reg)
    far_to = lax.rem(r + 2 - 4 * core + n_reg, n_reg)
    far_from = lax.rem(r - 2 + 4 * core + n_reg, n_reg)
    yp = lax.rem(y + 1, NT)
    yo = lax.rem(y + 2, NT)
    ym = lax.rem(y + 3, NT)

    count = [0]
    started = []

    def remote(src, dst, region, tm):
        i = count[0]
        count[0] += 1
        copy = pltpu.make_async_remote_copy(
            src_ref=src, dst_ref=dst, send_sem=send_sem.at[i], recv_sem=recv_sem.at[i],
            device_id=(region, tm), device_id_type=MESH)
        copy.start()
        started.append(copy)
        return copy

    t_copies = []
    for piece in range(4):
        rows = pl.ds(piece * (ROWS // 4), ROWS // 4)
        copy = pltpu.make_async_copy(t_hbm.at[rows], traw.at[rows], loc_sem.at[piece])
        t_copies.append(copy)
    g_copies = [
        pltpu.make_async_copy(go_hbm.at[0], gb.at[y, 0, 0], loc_sem.at[4]),
        pltpu.make_async_copy(gv_hbm.at[0], gb.at[y, 0, 1], loc_sem.at[5]),
    ]
    for copy in g_copies + t_copies:
        copy.start()

    barrier = pltpu.get_barrier_semaphore()
    for region in (inner, outer, far_to, far_from):
        pl.semaphore_signal(barrier, inc=1, device_id=(region, y), device_id_type=MESH)
    for tm in (yp, ym, yo):
        pl.semaphore_signal(barrier, inc=1, device_id=(r, tm), device_id_type=MESH)
    pl.semaphore_wait(barrier, 7)

    xo = [remote(g.at[0], gb.at[y, 1, i], outer, y) for i, g in enumerate((go_hbm, gv_hbm))]
    xf = [remote(g.at[0], gb.at[y, 2, i], far_to, y) for i, g in enumerate((go_hbm, gv_hbm))]
    y1a_p = [remote(g.at[0], gb.at[y, 0, i], r, yp) for i, g in enumerate((go_hbm, gv_hbm))]
    y1a_m = [remote(g.at[0], gb.at[y, 0, i], r, ym) for i, g in ((1, gv_hbm), (0, go_hbm))]
    xi = [remote(g.at[0], gb.at[y, 3, i], inner, y) for i, g in enumerate((go_hbm, gv_hbm))]
    offs = [remote(off_own, off_in, inner, y), remote(off_own, off_out, outer, y)]
    my_rows = pl.ds(pl.multiple_of(y * QROWS, QROWS), QROWS)

    def half_rows(half):
        return pl.ds(pl.multiple_of(half * 2 * HALF, 2 * HALF), 2 * HALF)


    xt_out = remote(t_hbm.at[my_rows, half_rows(core)], xr, outer, y)

    o_at = lax.broadcasted_iota(jnp.int32, (256, 256), 0)
    i_at = lax.broadcasted_iota(jnp.int32, (256, 256), 1)
    swap = ((lax.shift_right_logical(i_at, 4) == (o_at & 15))
            & ((i_at & 15) == lax.shift_right_logical(o_at, 4)))
    swap = jnp.where(swap, 1.0, 0.0).astype(BF16)

    def regroup(blocks):
        joined = jnp.concatenate([b.reshape(256, 128) for b in blocks], 1)
        moved = dot(swap, joined).astype(BF16)
        return [moved[:, i * 128:(i + 1) * 128] for i in range(len(blocks))]

    def own_rows(first, last):
        def step(p, carry):
            at = pl.ds(pl.multiple_of(p * 16, 16), 16)
            for pair in range(2):
                groups = (2 * pair, 2 * pair + 1)
                moved = regroup([traw[at, g * 16:(g + 1) * 16, :] for g in groups])
                for g, block in zip(groups, moved):
                    for q in range(16):
                        lane = (g * 8 + q // 2) * 256 + (q % 2) * 128
                        tt[at, lane:lane + 128] = block[q * 16:(q + 1) * 16]
            return carry
        lax.fori_loop(first, last, step, 0)

    def neighbour_rows():
        for qb in range(QROWS // 16):
            moved = regroup([xr[qb * 16:(qb + 1) * 16, g * 16:(g + 1) * 16, :] for g in range(2)])
            for g, block in enumerate(moved):
                for q in range(16):
                    row = (g * 8 + q // 2) * QROWS + qb * 16
                    lane = (q % 2) * 128
                    xt[row:row + 16, lane:lane + 128] = block[q * 16:(q + 1) * 16]

    places = (
        (off_own, 1 + 2 * core, 0, 3 - 2 * core),
        (off_in, 4 * core, 3, 4 - 4 * core),
        (off_out, 2 - 2 * core, 1, 2 * core),
    )

    def choose(j, place):
        off, before, here, after = places[place]
        down = jnp.broadcast_to(off[0:1, 0:1], (128, 128)) == -1
        up = jnp.broadcast_to(off[0:1, 1:2], (128, 128)) == 1
        for half in range(2):
            mid = gb[j, here, half].astype(F32)
            for slot, (mask, other) in enumerate(((down, before), (up, after))):
                got = jnp.where(mask, gb[j, other, half].astype(F32), mid).astype(BF16)
                at = slice(slot * 128, slot * 128 + 128)
                pk[place, at, half * 128:half * 128 + 128] = got
                if place == 0:
                    own_sw[j, at, (1 - half) * 128:(1 - half) * 128 + 128] = got

    def moments(j, place):
        choose(j, place)
        mm[place, j] = dot_t(pk[place], own_sw[j])

    def pick_time(column, j):
        w = jnp.float32(column[0])
        for k in range(1, NT):
            w = jnp.where(j == k, jnp.float32(column[k]), w)
        return w

    early = (y, ym, yp)

    def mix_early():
        rows_of_table = [[pick_time(TABLE[k], j) for j in early] for k in range(NT)]

        def step(c, carry):
            at = pl.ds(pl.multiple_of(c * 32, 32), 32)
            terms = [mm[2, j, at, :] for j in early]
            for k in range(NT):
                w = rows_of_table[k]
                part[k, at, :] = w[0] * terms[0] + w[1] * terms[1] + w[2] * terms[2]
            return carry
        lax.fori_loop(0, 8, step, 0)

    def mix_last():
        w = [pick_time(TABLE[k], yo) for k in range(NT)]

        def step(c, carry):
            at = pl.ds(pl.multiple_of(c * 32, 32), 32)
            last = mm[2, yo, at, :]
            for k in range(NT):
                nh[at, k * 256:(k + 1) * 256] = (part[k, at, :] + w[k] * last).astype(BF16)
            return carry
        lax.fori_loop(0, 8, step, 0)

    def mix_own(place):
        w = [pick_time([TABLE[k][j] for k in range(NT)], y) for j in range(NT)]

        def step(c, carry):
            at = pl.ds(pl.multiple_of(c * 32, 32), 32)
            total = w[0] * mm[place, 0, at, :]
            for j in range(1, NT):
                total = total + w[j] * mm[place, j, at, :]
            nd[at, :] = total.astype(BF16)
            return carry
        lax.fori_loop(0, 8, step, 0)

    for copy in g_copies:
        copy.wait()
    t_copies[0].wait()
    t_copies[1].wait()
    own_rows(0, 8)

    for copy in xo + xf:
        copy.wait_recv()
    y1b_p = [remote(gb.at[y, s], gb.at[y, s], r, yp) for s in (1, 2)]
    y1b_m = [remote(gb.at[y, s], gb.at[y, s], r, ym) for s in (2, 1)]
    in_y = remote(gb.at[y, 1], gb.at[y, 4], inner, y)

    y1a_p[0].wait_recv()
    y2a_p = remote(gb.at[ym, 0, 0], gb.at[ym, 0, 0], r, yp)
    y1a_m[0].wait_recv()
    y2a_m = remote(gb.at[yp, 0, 1], gb.at[yp, 0, 1], r, ym)
    y1a_p[1].wait_recv()
    y1a_m[1].wait_recv()
    in_m = [remote(gb.at[ym, 0], gb.at[ym, 3], inner, y)]
    in_p = [remote(gb.at[yp, 0], gb.at[yp, 3], inner, y)]

    t_copies[2].wait()
    t_copies[3].wait()
    own_rows(8, 11)

    y1b_p[0].wait_recv()
    y2b_p = remote(gb.at[ym, 1], gb.at[ym, 1], r, yp)
    in_m.append(remote(gb.at[ym, 1], gb.at[ym, 4], inner, y))
    y1b_m[0].wait_recv()
    y2b_m = remote(gb.at[yp, 2], gb.at[yp, 2], r, ym)
    y2a_p.wait_recv()
    y2a_m.wait_recv()
    in_o = [remote(gb.at[yo, 0], gb.at[yo, 3], inner, y)]
    y1b_p[1].wait_recv()
    y1b_m[1].wait_recv()
    in_p.append(remote(gb.at[yp, 1], gb.at[yp, 4], inner, y))

    for copy in xi + offs + [in_y]:
        copy.wait_recv()
    for place in range(3):
        moments(y, place)

    y2b_p.wait_recv()
    in_o.append(remote(gb.at[yo, 1], gb.at[yo, 4], inner, y))

    for copy in in_m + in_p:
        copy.wait_recv()
    for place in range(3):
        moments(ym, place)
        moments(yp, place)
    mix_early()
    own_rows(11, 16)
    lower = core * (HALF * 256)
    upper = (1 - core) * (HALF * 256)
    tin_copy = remote(tt.at[:, pl.ds(pl.multiple_of(upper, HALF * 256), HALF * 256)], tin, inner, y)
    xt_out.wait_recv()
    neighbour_rows()

    y2b_m.wait_recv()
    in_o[0].wait_recv()

    choose(yo, 0)
    moments(yo, 2)
    mix_last()

    def expand(g, carry):
        x = xt[pl.ds(pl.multiple_of(g * 256, 256), 256), :]
        for k in range(NT):
            got = dot(x, nh[:, k * 256:(k + 1) * 256]).astype(BF16)
            for m in range(4):
                lane = pl.ds(pl.multiple_of((g * 4 + m) * 256, 256), 256)
                v[k * QROWS:(k + 1) * QROWS, lane] = got[m * QROWS:(m + 1) * QROWS]
        return carry
    lax.fori_loop(0, 4, expand, 0)

    def times_own(first):
        acc[...] = jnp.zeros_like(acc)

        def step(g, carry):
            left = v[:, pl.ds(pl.multiple_of(g * 1024, 1024), 1024)]
            right = tt[:, pl.ds(pl.multiple_of(first + g * 1024, 1024), 1024)]
            acc[...] += dot_t(left, right)
            return carry
        lax.fori_loop(0, 4, step, 0)

    times_own(upper)
    for k in range(NT):
        pb[k] = acc[k * QROWS:(k + 1) * QROWS].astype(BF16)
    a2a = [remote(pb.at[t], ra.at[y], r, t) for t in (yp, ym, yo)]
    ex = [remote(pb.at[y], rb.at[y], outer, y)]
    ra[y] = pb[y]

    mm[0, yo] = dot_t(pk[0], own_sw[yo])
    mix_own(0)

    def make(buffer, source, g):
        for m in range(4):
            x = source[:, pl.ds(pl.multiple_of((g * 4 + m) * 256, 256), 256)]
            buffer[:, m * 256:(m + 1) * 256] = dot(x, nd[...]).astype(BF16)

    def use(buffer, total, first, g):
        right = tt[:, pl.ds(pl.multiple_of(first + g * 1024, 1024), 1024)]
        total[...] += dot_t(buffer[...], right)

    def head(source, total, first, groups):
        total[...] = jnp.zeros_like(total)
        make(ya, source, 0)

        def step(i, carry):
            make(yb, source, 2 * i + 1)
            use(ya, total, first, 2 * i)
            make(ya, source, 2 * i + 2)
            use(yb, total, first, 2 * i + 1)
            return carry
        lax.fori_loop(0, groups // 2 - 1, step, 0)

    def tail(source, total, first, groups):
        make(yb, source, groups - 1)
        use(ya, total, first, groups - 2)
        use(yb, total, first, groups - 1)

    head(tt, dfull, 0, MU // 4)

    for copy, t in zip(a2a, (ym, yp, yo)):
        copy.wait_recv()
        ex.append(remote(ra.at[t], rb.at[t], outer, y))
    tail(tt, dfull, 0, MU // 4)
    dfull[...] = 0.5 * (dfull[...] + dfull[...].T)
    db[...] = dfull[...].astype(BF16)
    dx = [remote(db, dn.at[0], inner, y), remote(db, dn.at[1], outer, y)]

    in_o[1].wait_recv()
    moments(yo, 1)
    mix_own(1)
    tin_copy.wait_recv()

    head(tin, acc, lower, HALF // 4)
    tail(tin, acc, lower, HALF // 4)
    pin[...] = acc[...].astype(BF16)
    ex_in = remote(pin, rin, inner, y)
    turned[0] = acc[...].T
    turned[1] = ra[...].reshape(ROWS, ROWS).astype(F32).T

    d_high, d_low = split(dfull[...])
    diag = dfull[...] + dot(d_high, d_high) + dot(d_high, d_low) + dot(d_low, d_high)
    for side in (1, 0):
        dx[side].wait_recv()
        if side == 1:
            for copy in ex:
                copy.wait_recv()
            came = rb[...].reshape(ROWS, ROWS)
        else:
            ex_in.wait_recv()
            came = rin[...]
        place = (2 - 2 * core) if side == 0 else 2 * core
        keep = pat[0, place].astype(F32)
        block = keep * (came.astype(F32) + turned[side])
        high, low = split(block)
        diag = diag + dot_t(high, high) + dot_t(high, low) + dot_t(low, high)
        result = (block + dot(d_high, high) + dot(d_high, low) + dot(d_low, high)
                  + dot(high, dn[side]) + dot(low, dn[side]))
        out_ref[0, :, pl.ds(pl.multiple_of(place * ROWS, ROWS), ROWS)] = keep * result
    out_ref[0, :, ROWS:2 * ROWS] = pat[0, 1].astype(F32) * diag

    for copy in started:
        copy.wait_send()


COPIES = 48


def local(n_reg, tensor, g_occ, g_virt, offsets, pattern):
    anyspace = pl.BlockSpec(memory_space=pl.ANY)
    vmem = pl.BlockSpec(memory_space=pltpu.VMEM)
    return pl.pallas_call(
        functools.partial(kernel, n_reg),
        out_shape=pltpu.VMEM((1, ROWS, 3 * ROWS), F32),
        in_specs=[anyspace, anyspace, anyspace, vmem, pl.BlockSpec(memory_space=pltpu.SMEM)],
        out_specs=vmem,
        scratch_shapes=[
            pltpu.VMEM((ROWS, 2 * MU, NU), BF16),
            pltpu.VMEM((ROWS, MU * 256), BF16),
            pltpu.VMEM((ROWS, HALF * 256), BF16),
            pltpu.VMEM((QROWS, 2 * HALF, NU), BF16),
            pltpu.VMEM((HALF * QROWS, 256), BF16),
            pltpu.VMEM((NT, 5, 2, NU, LAM), BF16),
            pltpu.VMEM((1, 2), jnp.int32),
            pltpu.VMEM((1, 2), jnp.int32),
            pltpu.VMEM((3, 256, 256), BF16),
            pltpu.VMEM((NT, 256, 256), BF16),
            pltpu.VMEM((3, NT, 256, 256), F32),
            pltpu.VMEM((NT, 256, 256), F32),
            pltpu.VMEM((256, NT * 256), BF16),
            pltpu.VMEM((256, 256), BF16),
            pltpu.VMEM((NT * QROWS, HALF * 256), BF16),
            pltpu.VMEM((256, 256), F32),
            pltpu.VMEM((NT, QROWS, 256), BF16),
            pltpu.VMEM((NT, QROWS, 256), BF16),
            pltpu.VMEM((NT, QROWS, 256), BF16),
            pltpu.VMEM((ROWS, ROWS), BF16),
            pltpu.VMEM((ROWS, ROWS), BF16),
            pltpu.VMEM((2, ROWS, ROWS), F32),
            pltpu.VMEM((256, 256), BF16),
            pltpu.VMEM((2, 256, 256), BF16),
            pltpu.VMEM((256, 256), F32),
            pltpu.VMEM((256, 1024), BF16),
            pltpu.VMEM((256, 1024), BF16),
            pltpu.SemaphoreType.DMA((6,)),
            pltpu.SemaphoreType.DMA((COPIES,)),
            pltpu.SemaphoreType.DMA((COPIES,)),
        ],
        compiler_params=pltpu.CompilerParams(collective_id=0, has_side_effects=True),
        name="screen",
    )(tensor.reshape(ROWS, 2 * MU, NU), g_occ, g_virt, offsets, pattern)


def solution(mesh):
    return jax.shard_map(
        functools.partial(local, mesh.shape["region"]),
        mesh=mesh,
        in_specs=(
            P("region", None, None, None),
            P("tm", "region", None),
            P("tm", "region", None),
            P("region", None),
            P("region", None),
        ),
        out_specs=P("tm", "region", None),
        check_vma=False,
    )
```

```python
import functools
import math

import jax
import jax.numpy as jnp
from jax import lax
from jax.experimental import pallas as pl
from jax.experimental.pallas import tpu as pltpu
from jax.sharding import PartitionSpec as P

MESH = pl.DeviceIdType.MESH
F32 = jnp.float32
BF16 = jnp.bfloat16

time_points = (0.1, 0.5, 1.5, 4.0)
time_weights = (0.2, 0.6, 1.2, 2.5)
omega_points = (0.2, 0.9, 2.5, 7.0)
NT = 4
ROWS = 256
MU = 32
NU = 128
LAM = 128
HALF = MU // 2
QROWS = ROWS // NT
PREFACTOR = 1.0 / math.sqrt(2.0 * MU * LAM) / (3.0 * ROWS) ** 0.25
TABLE = [
    [PREFACTOR * w * math.cos(om * t) for t, w in zip(time_points, time_weights)]
    for om in omega_points
]


def dot(a, b):
    return jnp.dot(a, b, preferred_element_type=F32)


def dot_t(a, b):
    return lax.dot_general(a, b, (((1,), (1,)), ((), ())), preferred_element_type=F32)


def split(x):
    high = x.astype(BF16)
    return high, (x - high.astype(F32)).astype(BF16)


def kernel(n_reg, t_hbm, go_hbm, gv_hbm, off_own, pat, out_ref,
           traw, tt, tin, xr, xt, gb, off_in, off_out, pk, own_sw, mm, part, nh, nd, v,
           acc, pb, ra, rb, pin, rin, turned, db, dn, dfull, ya, yb, loc_sem, send_sem, recv_sem):
    r = lax.axis_index("region")
    y = lax.axis_index("tm")
    core = lax.rem(r, 2)
    inner = r + 1 - 2 * core
    outer = lax.rem(r - 1 + 2 * core + n_reg, n_reg)
    far_to = lax.rem(r + 2 - 4 * core + n_reg, n_reg)
    far_from = lax.rem(r - 2 + 4 * core + n_reg, n_reg)
    yp = lax.rem(y + 1, NT)
    yo = lax.rem(y + 2, NT)
    ym = lax.rem(y + 3, NT)

    count = [0]
    started = []

    def remote(src, dst, region, tm):
        i = count[0]
        count[0] += 1
        copy = pltpu.make_async_remote_copy(
            src_ref=src, dst_ref=dst, send_sem=send_sem.at[i], recv_sem=recv_sem.at[i],
            device_id=(region, tm), device_id_type=MESH)
        copy.start()
        started.append(copy)
        return copy

    t_copies = []
    for piece in range(4):
        rows = pl.ds(piece * (ROWS // 4), ROWS // 4)
        copy = pltpu.make_async_copy(t_hbm.at[rows], traw.at[rows], loc_sem.at[piece])
        t_copies.append(copy)
    g_copies = [
        pltpu.make_async_copy(go_hbm.at[0], gb.at[y, 0, 0], loc_sem.at[4]),
        pltpu.make_async_copy(gv_hbm.at[0], gb.at[y, 0, 1], loc_sem.at[5]),
    ]
    for copy in g_copies + t_copies:
        copy.start()

    barrier = pltpu.get_barrier_semaphore()
    for region in (inner, outer, far_to, far_from):
        pl.semaphore_signal(barrier, inc=1, device_id=(region, y), device_id_type=MESH)
    for tm in (yp, ym, yo):
        pl.semaphore_signal(barrier, inc=1, device_id=(r, tm), device_id_type=MESH)
    pl.semaphore_wait(barrier, 7)

    xo = [remote(g.at[0], gb.at[y, 1, i], outer, y) for i, g in enumerate((go_hbm, gv_hbm))]
    xf = [remote(g.at[0], gb.at[y, 2, i], far_to, y) for i, g in enumerate((go_hbm, gv_hbm))]
    y1a_p = [remote(g.at[0], gb.at[y, 0, i], r, yp) for i, g in enumerate((go_hbm, gv_hbm))]
    y1a_m = [remote(g.at[0], gb.at[y, 0, i], r, ym) for i, g in ((1, gv_hbm), (0, go_hbm))]
    xi = [remote(g.at[0], gb.at[y, 3, i], inner, y) for i, g in enumerate((go_hbm, gv_hbm))]
    offs = [remote(off_own, off_in, inner, y), remote(off_own, off_out, outer, y)]
    my_rows = pl.ds(pl.multiple_of(y * QROWS, QROWS), QROWS)

    def half_rows(half):
        return pl.ds(pl.multiple_of(half * 2 * HALF, 2 * HALF), 2 * HALF)


    o_at = lax.broadcasted_iota(jnp.int32, (256, 256), 0)
    i_at = lax.broadcasted_iota(jnp.int32, (256, 256), 1)
    swap = ((lax.shift_right_logical(i_at, 4) == (o_at & 15))
            & ((i_at & 15) == lax.shift_right_logical(o_at, 4)))
    swap = jnp.where(swap, 1.0, 0.0).astype(BF16)

    def regroup(blocks):
        joined = jnp.concatenate([b.reshape(256, 128) for b in blocks], 1)
        moved = dot(swap, joined).astype(BF16)
        return [moved[:, i * 128:(i + 1) * 128] for i in range(len(blocks))]

    def own_rows(first, last):
        def step(p, carry):
            at = pl.ds(pl.multiple_of(p * 16, 16), 16)
            for pair in range(2):
                groups = (2 * pair, 2 * pair + 1)
                moved = regroup([traw[at, g * 16:(g + 1) * 16, :] for g in groups])
                for g, block in zip(groups, moved):
                    for q in range(16):
                        lane = (g * 8 + q // 2) * 256 + (q % 2) * 128
                        tt[at, lane:lane + 128] = block[q * 16:(q + 1) * 16]
            return carry
        lax.fori_loop(first, last, step, 0)

    def neighbour_rows():
        for qb in range(QROWS // 16):
            moved = regroup([xr[qb * 16:(qb + 1) * 16, g * 16:(g + 1) * 16, :] for g in range(2)])
            for g, block in enumerate(moved):
                for q in range(16):
                    row = (g * 8 + q // 2) * QROWS + qb * 16
                    lane = (q % 2) * 128
                    xt[row:row + 16, lane:lane + 128] = block[q * 16:(q + 1) * 16]

    places = (
        (off_own, 1 + 2 * core, 0, 3 - 2 * core),
        (off_in, 4 * core, 3, 4 - 4 * core),
        (off_out, 2 - 2 * core, 1, 2 * core),
    )

    def choose(j, place):
        off, before, here, after = places[place]
        down = jnp.broadcast_to(off[0:1, 0:1], (128, 128)) == -1
        up = jnp.broadcast_to(off[0:1, 1:2], (128, 128)) == 1
        for half in range(2):
            mid = gb[j, here, half].astype(F32)
            for slot, (mask, other) in enumerate(((down, before), (up, after))):
                got = jnp.where(mask, gb[j, other, half].astype(F32), mid).astype(BF16)
                at = slice(slot * 128, slot * 128 + 128)
                pk[place, at, half * 128:half * 128 + 128] = got
                if place == 0:
                    own_sw[j, at, (1 - half) * 128:(1 - half) * 128 + 128] = got

    def moments(j, place):
        choose(j, place)
        mm[place, j] = dot_t(pk[place], own_sw[j])

    def pick_time(column, j):
        w = jnp.float32(column[0])
        for k in range(1, NT):
            w = jnp.where(j == k, jnp.float32(column[k]), w)
        return w

    early = (y, ym, yp)

    def mix_early():
        rows_of_table = [[pick_time(TABLE[k], j) for j in early] for k in range(NT)]

        def step(c, carry):
            at = pl.ds(pl.multiple_of(c * 32, 32), 32)
            terms = [mm[2, j, at, :] for j in early]
            for k in range(NT):
                w = rows_of_table[k]
                part[k, at, :] = w[0] * terms[0] + w[1] * terms[1] + w[2] * terms[2]
            return carry
        lax.fori_loop(0, 8, step, 0)

    def mix_last():
        w = [pick_time(TABLE[k], yo) for k in range(NT)]

        def step(c, carry):
            at = pl.ds(pl.multiple_of(c * 32, 32), 32)
            last = mm[2, yo, at, :]
            for k in range(NT):
                nh[at, k * 256:(k + 1) * 256] = (part[k, at, :] + w[k] * last).astype(BF16)
            return carry
        lax.fori_loop(0, 8, step, 0)

    def mix_own(place):
        w = [pick_time([TABLE[k][j] for k in range(NT)], y) for j in range(NT)]

        def step(c, carry):
            at = pl.ds(pl.multiple_of(c * 32, 32), 32)
            total = w[0] * mm[place, 0, at, :]
            for j in range(1, NT):
                total = total + w[j] * mm[place, j, at, :]
            nd[at, :] = total.astype(BF16)
            return carry
        lax.fori_loop(0, 8, step, 0)

    for copy in g_copies:
        copy.wait()
    t_copies[0].wait()
    own_rows(0, 4)
    xt_out = remote(t_hbm.at[my_rows, half_rows(core)], xr, outer, y)
    t_copies[1].wait()
    own_rows(4, 8)

    for copy in xo + xf:
        copy.wait_recv()
    y1b_p = [remote(gb.at[y, s], gb.at[y, s], r, yp) for s in (1, 2)]
    y1b_m = [remote(gb.at[y, s], gb.at[y, s], r, ym) for s in (2, 1)]
    in_y = remote(gb.at[y, 1], gb.at[y, 4], inner, y)

    y1a_p[0].wait_recv()
    y2a_p = remote(gb.at[ym, 0, 0], gb.at[ym, 0, 0], r, yp)
    y1a_m[0].wait_recv()
    y2a_m = remote(gb.at[yp, 0, 1], gb.at[yp, 0, 1], r, ym)
    y1a_p[1].wait_recv()
    y1a_m[1].wait_recv()
    in_m = [remote(gb.at[ym, 0], gb.at[ym, 3], inner, y)]
    in_p = [remote(gb.at[yp, 0], gb.at[yp, 3], inner, y)]

    t_copies[2].wait()
    t_copies[3].wait()
    own_rows(8, 16)
    lower = core * (HALF * 256)
    upper = (1 - core) * (HALF * 256)
    tin_copy = remote(tt.at[:, pl.ds(pl.multiple_of(upper, HALF * 256), HALF * 256)], tin, inner, y)

    y1b_p[0].wait_recv()
    y2b_p = remote(gb.at[ym, 1], gb.at[ym, 1], r, yp)
    in_m.append(remote(gb.at[ym, 1], gb.at[ym, 4], inner, y))
    y1b_m[0].wait_recv()
    y2b_m = remote(gb.at[yp, 2], gb.at[yp, 2], r, ym)
    y2a_p.wait_recv()
    y2a_m.wait_recv()
    in_o = [remote(gb.at[yo, 0], gb.at[yo, 3], inner, y)]
    y1b_p[1].wait_recv()
    y1b_m[1].wait_recv()
    in_p.append(remote(gb.at[yp, 1], gb.at[yp, 4], inner, y))

    for copy in xi + offs + [in_y]:
        copy.wait_recv()
    for place in range(3):
        moments(y, place)

    in_m[0].wait_recv()
    in_p[0].wait_recv()
    for place in (0, 2):
        moments(ym, place)
        moments(yp, place)
    mix_early()
    y2b_p.wait_recv()
    in_o.append(remote(gb.at[yo, 1], gb.at[yo, 4], inner, y))
    xt_out.wait_recv()
    neighbour_rows()
    in_m[1].wait_recv()
    in_p[1].wait_recv()
    moments(ym, 1)
    moments(yp, 1)

    y2b_m.wait_recv()
    in_o[0].wait_recv()

    choose(yo, 0)
    moments(yo, 2)
    mix_last()

    def expand(g, carry):
        x = xt[pl.ds(pl.multiple_of(g * 256, 256), 256), :]
        for k in range(NT):
            got = dot(x, nh[:, k * 256:(k + 1) * 256]).astype(BF16)
            for m in range(4):
                lane = pl.ds(pl.multiple_of((g * 4 + m) * 256, 256), 256)
                v[k * QROWS:(k + 1) * QROWS, lane] = got[m * QROWS:(m + 1) * QROWS]
        return carry
    lax.fori_loop(0, 4, expand, 0)

    def times_own(first):
        acc[...] = jnp.zeros_like(acc)

        def step(g, carry):
            left = v[:, pl.ds(pl.multiple_of(g * 1024, 1024), 1024)]
            right = tt[:, pl.ds(pl.multiple_of(first + g * 1024, 1024), 1024)]
            acc[...] += dot_t(left, right)
            return carry
        lax.fori_loop(0, 4, step, 0)

    times_own(upper)
    for k in range(NT):
        pb[k] = acc[k * QROWS:(k + 1) * QROWS].astype(BF16)
    a2a = [remote(pb.at[t], ra.at[y], r, t) for t in (yp, ym, yo)]
    ex = [remote(pb.at[y], rb.at[y], outer, y)]
    ra[y] = pb[y]

    mm[0, yo] = dot_t(pk[0], own_sw[yo])
    mix_own(0)

    def make(buffer, source, g):
        for m in range(4):
            x = source[:, pl.ds(pl.multiple_of((g * 4 + m) * 256, 256), 256)]
            buffer[:, m * 256:(m + 1) * 256] = dot(x, nd[...]).astype(BF16)

    def use(buffer, total, first, g):
        right = tt[:, pl.ds(pl.multiple_of(first + g * 1024, 1024), 1024)]
        total[...] += dot_t(buffer[...], right)

    def head(source, total, first, groups):
        total[...] = jnp.zeros_like(total)
        make(ya, source, 0)

        def step(i, carry):
            make(yb, source, 2 * i + 1)
            use(ya, total, first, 2 * i)
            make(ya, source, 2 * i + 2)
            use(yb, total, first, 2 * i + 1)
            return carry
        lax.fori_loop(0, groups // 2 - 1, step, 0)

    def tail(source, total, first, groups):
        make(yb, source, groups - 1)
        use(ya, total, first, groups - 2)
        use(yb, total, first, groups - 1)

    head(tt, dfull, 0, MU // 4)

    tail(tt, dfull, 0, MU // 4)

    for copy, t in zip(a2a, (ym, yp, yo)):
        copy.wait_recv()
        ex.append(remote(ra.at[t], rb.at[t], outer, y))
    dfull[...] = 0.5 * (dfull[...] + dfull[...].T)
    db[...] = dfull[...].astype(BF16)
    dx = [remote(db, dn.at[0], inner, y), remote(db, dn.at[1], outer, y)]

    in_o[1].wait_recv()
    moments(yo, 1)
    mix_own(1)
    tin_copy.wait_recv()

    head(tin, acc, lower, HALF // 4)
    tail(tin, acc, lower, HALF // 4)
    pin[...] = acc[...].astype(BF16)
    ex_in = remote(pin, rin, inner, y)
    turned[0] = acc[...].T
    turned[1] = ra[...].reshape(ROWS, ROWS).astype(F32).T

    d_high, d_low = split(dfull[...])
    diag = dfull[...] + dot(d_high, d_high) + dot(d_high, d_low) + dot(d_low, d_high)
    for side in (1, 0):
        dx[side].wait_recv()
        if side == 1:
            for copy in ex:
                copy.wait_recv()
            came = rb[...].reshape(ROWS, ROWS)
        else:
            ex_in.wait_recv()
            came = rin[...]
        place = (2 - 2 * core) if side == 0 else 2 * core
        keep = pat[0, place].astype(F32)
        block = keep * (came.astype(F32) + turned[side])
        high, low = split(block)
        diag = diag + dot_t(high, high) + dot_t(high, low) + dot_t(low, high)
        result = (block + dot(d_high, high) + dot(d_high, low) + dot(d_low, high)
                  + dot(high, dn[side]) + dot(low, dn[side]))
        out_ref[0, :, pl.ds(pl.multiple_of(place * ROWS, ROWS), ROWS)] = keep * result
    out_ref[0, :, ROWS:2 * ROWS] = pat[0, 1].astype(F32) * diag

    for copy in started:
        copy.wait_send()


COPIES = 48


def local(n_reg, tensor, g_occ, g_virt, offsets, pattern):
    anyspace = pl.BlockSpec(memory_space=pl.ANY)
    vmem = pl.BlockSpec(memory_space=pltpu.VMEM)
    return pl.pallas_call(
        functools.partial(kernel, n_reg),
        out_shape=pltpu.VMEM((1, ROWS, 3 * ROWS), F32),
        in_specs=[anyspace, anyspace, anyspace, vmem, pl.BlockSpec(memory_space=pltpu.SMEM)],
        out_specs=vmem,
        scratch_shapes=[
            pltpu.VMEM((ROWS, 2 * MU, NU), BF16),
            pltpu.VMEM((ROWS, MU * 256), BF16),
            pltpu.VMEM((ROWS, HALF * 256), BF16),
            pltpu.VMEM((QROWS, 2 * HALF, NU), BF16),
            pltpu.VMEM((HALF * QROWS, 256), BF16),
            pltpu.VMEM((NT, 5, 2, NU, LAM), BF16),
            pltpu.VMEM((1, 2), jnp.int32),
            pltpu.VMEM((1, 2), jnp.int32),
            pltpu.VMEM((3, 256, 256), BF16),
            pltpu.VMEM((NT, 256, 256), BF16),
            pltpu.VMEM((3, NT, 256, 256), F32),
            pltpu.VMEM((NT, 256, 256), F32),
            pltpu.VMEM((256, NT * 256), BF16),
            pltpu.VMEM((256, 256), BF16),
            pltpu.VMEM((NT * QROWS, HALF * 256), BF16),
            pltpu.VMEM((256, 256), F32),
            pltpu.VMEM((NT, QROWS, 256), BF16),
            pltpu.VMEM((NT, QROWS, 256), BF16),
            pltpu.VMEM((NT, QROWS, 256), BF16),
            pltpu.VMEM((ROWS, ROWS), BF16),
            pltpu.VMEM((ROWS, ROWS), BF16),
            pltpu.VMEM((2, ROWS, ROWS), F32),
            pltpu.VMEM((256, 256), BF16),
            pltpu.VMEM((2, 256, 256), BF16),
            pltpu.VMEM((256, 256), F32),
            pltpu.VMEM((256, 1024), BF16),
            pltpu.VMEM((256, 1024), BF16),
            pltpu.SemaphoreType.DMA((6,)),
            pltpu.SemaphoreType.DMA((COPIES,)),
            pltpu.SemaphoreType.DMA((COPIES,)),
        ],
        compiler_params=pltpu.CompilerParams(collective_id=0, has_side_effects=True),
        name="screen",
    )(tensor.reshape(ROWS, 2 * MU, NU), g_occ, g_virt, offsets, pattern)


def solution(mesh):
    return jax.shard_map(
        functools.partial(local, mesh.shape["region"]),
        mesh=mesh,
        in_specs=(
            P("region", None, None, None),
            P("tm", "region", None),
            P("tm", "region", None),
            P("region", None),
            P("region", None),
        ),
        out_specs=P("tm", "region", None),
        check_vma=False,
    )
```

```python
import functools
import math

import jax
import jax.numpy as jnp
from jax import lax
from jax.experimental import pallas as pl
from jax.experimental.pallas import tpu as pltpu
from jax.sharding import PartitionSpec as P

MESH = pl.DeviceIdType.MESH
F32 = jnp.float32
BF16 = jnp.bfloat16

time_points = (0.1, 0.5, 1.5, 4.0)
time_weights = (0.2, 0.6, 1.2, 2.5)
omega_points = (0.2, 0.9, 2.5, 7.0)
NT = 4
ROWS = 256
MU = 32
NU = 128
LAM = 128
HALF = MU // 2
QROWS = ROWS // NT
PREFACTOR = 1.0 / math.sqrt(2.0 * MU * LAM) / (3.0 * ROWS) ** 0.25
TABLE = [
    [PREFACTOR * w * math.cos(om * t) for t, w in zip(time_points, time_weights)]
    for om in omega_points
]


def dot(a, b):
    return jnp.dot(a, b, preferred_element_type=F32)


def dot_t(a, b):
    return lax.dot_general(a, b, (((1,), (1,)), ((), ())), preferred_element_type=F32)


def split(x):
    high = x.astype(BF16)
    return high, (x - high.astype(F32)).astype(BF16)


def kernel(n_reg, t_hbm, go_hbm, gv_hbm, off_own, pat, out_ref,
           traw, tt, tin, xr, xt, gb, off_in, off_out, pk, own_sw, mm, part, nh, nd,
           acc, pb, ra, rb, pin, rin, turned, db, dn, dfull, ya, yb, loc_sem, send_sem, recv_sem):
    r = lax.axis_index("region")
    y = lax.axis_index("tm")
    core = lax.rem(r, 2)
    inner = r + 1 - 2 * core
    outer = lax.rem(r - 1 + 2 * core + n_reg, n_reg)
    far_to = lax.rem(r + 2 - 4 * core + n_reg, n_reg)
    far_from = lax.rem(r - 2 + 4 * core + n_reg, n_reg)
    yp = lax.rem(y + 1, NT)
    yo = lax.rem(y + 2, NT)
    ym = lax.rem(y + 3, NT)

    count = [0]
    started = []

    def remote(src, dst, region, tm):
        i = count[0]
        count[0] += 1
        copy = pltpu.make_async_remote_copy(
            src_ref=src, dst_ref=dst, send_sem=send_sem.at[i], recv_sem=recv_sem.at[i],
            device_id=(region, tm), device_id_type=MESH)
        copy.start()
        started.append(copy)
        return copy

    t_copies = []
    for piece in range(4):
        rows = pl.ds(piece * (ROWS // 4), ROWS // 4)
        copy = pltpu.make_async_copy(t_hbm.at[rows], traw.at[rows], loc_sem.at[piece])
        t_copies.append(copy)
    g_copies = [
        pltpu.make_async_copy(go_hbm.at[0], gb.at[y, 0, 0], loc_sem.at[4]),
        pltpu.make_async_copy(gv_hbm.at[0], gb.at[y, 0, 1], loc_sem.at[5]),
    ]
    for copy in g_copies + t_copies:
        copy.start()

    barrier = pltpu.get_barrier_semaphore()
    for region in (inner, outer, far_to, far_from):
        pl.semaphore_signal(barrier, inc=1, device_id=(region, y), device_id_type=MESH)
    for tm in (yp, ym, yo):
        pl.semaphore_signal(barrier, inc=1, device_id=(r, tm), device_id_type=MESH)
    pl.semaphore_wait(barrier, 7)

    xo = [remote(g.at[0], gb.at[y, 1, i], outer, y) for i, g in enumerate((go_hbm, gv_hbm))]
    xf = [remote(g.at[0], gb.at[y, 2, i], far_to, y) for i, g in enumerate((go_hbm, gv_hbm))]
    y1a_p = [remote(g.at[0], gb.at[y, 0, i], r, yp) for i, g in enumerate((go_hbm, gv_hbm))]
    y1a_m = [remote(g.at[0], gb.at[y, 0, i], r, ym) for i, g in ((1, gv_hbm), (0, go_hbm))]
    xi = [remote(g.at[0], gb.at[y, 3, i], inner, y) for i, g in enumerate((go_hbm, gv_hbm))]
    offs = [remote(off_own, off_in, inner, y), remote(off_own, off_out, outer, y)]
    my_rows = pl.ds(pl.multiple_of(y * QROWS, QROWS), QROWS)

    def half_rows(half):
        return pl.ds(pl.multiple_of(half * 2 * HALF, 2 * HALF), 2 * HALF)


    o_at = lax.broadcasted_iota(jnp.int32, (256, 256), 0)
    i_at = lax.broadcasted_iota(jnp.int32, (256, 256), 1)
    swap = ((lax.shift_right_logical(i_at, 4) == (o_at & 15))
            & ((i_at & 15) == lax.shift_right_logical(o_at, 4)))
    swap = jnp.where(swap, 1.0, 0.0).astype(BF16)

    def regroup(blocks):
        joined = jnp.concatenate([b.reshape(256, 128) for b in blocks], 1)
        moved = dot(swap, joined).astype(BF16)
        return [moved[:, i * 128:(i + 1) * 128] for i in range(len(blocks))]

    def own_rows(first, last):
        def step(p, carry):
            at = pl.ds(pl.multiple_of(p * 16, 16), 16)
            for pair in range(2):
                groups = (2 * pair, 2 * pair + 1)
                moved = regroup([traw[at, g * 16:(g + 1) * 16, :] for g in groups])
                for g, block in zip(groups, moved):
                    for q in range(16):
                        lane = (g * 8 + q // 2) * 256 + (q % 2) * 128
                        tt[at, lane:lane + 128] = block[q * 16:(q + 1) * 16]
            return carry
        lax.fori_loop(first, last, step, 0)

    def neighbour_rows():
        for qb in range(QROWS // 16):
            moved = regroup([xr[qb * 16:(qb + 1) * 16, g * 16:(g + 1) * 16, :] for g in range(2)])
            for g, block in enumerate(moved):
                for q in range(16):
                    row = (g * 8 + q // 2) * QROWS + qb * 16
                    lane = (q % 2) * 128
                    xt[row:row + 16, lane:lane + 128] = block[q * 16:(q + 1) * 16]

    places = (
        (off_own, 1 + 2 * core, 0, 3 - 2 * core),
        (off_in, 4 * core, 3, 4 - 4 * core),
        (off_out, 2 - 2 * core, 1, 2 * core),
    )

    def choose(j, place):
        off, before, here, after = places[place]
        down = jnp.broadcast_to(off[0:1, 0:1], (128, 128)) == -1
        up = jnp.broadcast_to(off[0:1, 1:2], (128, 128)) == 1
        for half in range(2):
            mid = gb[j, here, half].astype(F32)
            for slot, (mask, other) in enumerate(((down, before), (up, after))):
                got = jnp.where(mask, gb[j, other, half].astype(F32), mid).astype(BF16)
                at = slice(slot * 128, slot * 128 + 128)
                pk[place, at, half * 128:half * 128 + 128] = got
                if place == 0:
                    own_sw[j, at, (1 - half) * 128:(1 - half) * 128 + 128] = got

    def moments(j, place):
        choose(j, place)
        mm[place, j] = dot_t(pk[place], own_sw[j])

    def pick_time(column, j):
        w = jnp.float32(column[0])
        for k in range(1, NT):
            w = jnp.where(j == k, jnp.float32(column[k]), w)
        return w

    early = (y, ym, yp)

    def mix_early():
        rows_of_table = [[pick_time(TABLE[k], j) for j in early] for k in range(NT)]

        def step(c, carry):
            at = pl.ds(pl.multiple_of(c * 32, 32), 32)
            terms = [mm[2, j, at, :] for j in early]
            for k in range(NT):
                w = rows_of_table[k]
                part[k, at, :] = w[0] * terms[0] + w[1] * terms[1] + w[2] * terms[2]
            return carry
        lax.fori_loop(0, 8, step, 0)

    def mix_last():
        w = [pick_time(TABLE[k], yo) for k in range(NT)]

        def step(c, carry):
            at = pl.ds(pl.multiple_of(c * 32, 32), 32)
            last = mm[2, yo, at, :]
            for k in range(NT):
                nh[at, k * 256:(k + 1) * 256] = (part[k, at, :] + w[k] * last).astype(BF16)
            return carry
        lax.fori_loop(0, 8, step, 0)

    def mix_own(place):
        w = [pick_time([TABLE[k][j] for k in range(NT)], y) for j in range(NT)]

        def step(c, carry):
            at = pl.ds(pl.multiple_of(c * 32, 32), 32)
            total = w[0] * mm[place, 0, at, :]
            for j in range(1, NT):
                total = total + w[j] * mm[place, j, at, :]
            nd[at, :] = total.astype(BF16)
            return carry
        lax.fori_loop(0, 8, step, 0)

    for copy in g_copies:
        copy.wait()
    t_copies[0].wait()
    own_rows(0, 4)
    xt_out = remote(t_hbm.at[my_rows, half_rows(core)], xr, outer, y)
    t_copies[1].wait()
    own_rows(4, 8)

    for copy in xo + xf:
        copy.wait_recv()
    y1b_p = [remote(gb.at[y, s], gb.at[y, s], r, yp) for s in (1, 2)]
    y1b_m = [remote(gb.at[y, s], gb.at[y, s], r, ym) for s in (2, 1)]
    in_y = remote(gb.at[y, 1], gb.at[y, 4], inner, y)

    y1a_p[0].wait_recv()
    y2a_p = remote(gb.at[ym, 0, 0], gb.at[ym, 0, 0], r, yp)
    y1a_m[0].wait_recv()
    y2a_m = remote(gb.at[yp, 0, 1], gb.at[yp, 0, 1], r, ym)
    y1a_p[1].wait_recv()
    y1a_m[1].wait_recv()
    in_m = [remote(gb.at[ym, 0], gb.at[ym, 3], inner, y)]
    in_p = [remote(gb.at[yp, 0], gb.at[yp, 3], inner, y)]

    t_copies[2].wait()
    t_copies[3].wait()
    own_rows(8, 16)
    lower = core * (HALF * 256)
    upper = (1 - core) * (HALF * 256)
    tin_copy = remote(tt.at[:, pl.ds(pl.multiple_of(upper, HALF * 256), HALF * 256)], tin, inner, y)

    y1b_p[0].wait_recv()
    y2b_p = remote(gb.at[ym, 1], gb.at[ym, 1], r, yp)
    in_m.append(remote(gb.at[ym, 1], gb.at[ym, 4], inner, y))
    y1b_m[0].wait_recv()
    y2b_m = remote(gb.at[yp, 2], gb.at[yp, 2], r, ym)
    y2a_p.wait_recv()
    y2a_m.wait_recv()
    in_o = [remote(gb.at[yo, 0], gb.at[yo, 3], inner, y)]
    y1b_p[1].wait_recv()
    y1b_m[1].wait_recv()
    in_p.append(remote(gb.at[yp, 1], gb.at[yp, 4], inner, y))

    for copy in xi + offs + [in_y]:
        copy.wait_recv()
    for place in range(3):
        moments(y, place)

    in_m[0].wait_recv()
    in_p[0].wait_recv()
    for place in (0, 2):
        moments(ym, place)
        moments(yp, place)
    mix_early()
    y2b_p.wait_recv()
    in_o.append(remote(gb.at[yo, 1], gb.at[yo, 4], inner, y))
    xt_out.wait_recv()
    neighbour_rows()
    in_m[1].wait_recv()
    in_p[1].wait_recv()
    moments(ym, 1)
    moments(yp, 1)

    y2b_m.wait_recv()
    in_o[0].wait_recv()

    choose(yo, 0)
    moments(yo, 2)
    mix_last()

    def from_rows(source):
        def make(buffer, g):
            for m in range(4):
                x = source[:, pl.ds(pl.multiple_of((g * 4 + m) * 256, 256), 256)]
                buffer[:, m * 256:(m + 1) * 256] = dot(x, nd[...]).astype(BF16)
        return make

    def from_slices(buffer, g):
        x = xt[pl.ds(pl.multiple_of(g * 256, 256), 256), :]
        for k in range(NT):
            got = dot(x, nh[:, k * 256:(k + 1) * 256]).astype(BF16)
            for m in range(4):
                buffer[k * QROWS:(k + 1) * QROWS, m * 256:(m + 1) * 256] = got[m * QROWS:(m + 1) * QROWS]

    def use(buffer, total, first, g):
        right = tt[:, pl.ds(pl.multiple_of(first + g * 1024, 1024), 1024)]
        total[...] += dot_t(buffer[...], right)

    def head(make, total, first, groups):
        total[...] = jnp.zeros_like(total)
        make(ya, 0)

        def step(i, carry):
            make(yb, 2 * i + 1)
            use(ya, total, first, 2 * i)
            make(ya, 2 * i + 2)
            use(yb, total, first, 2 * i + 1)
            return carry
        lax.fori_loop(0, groups // 2 - 1, step, 0)

    def tail(make, total, first, groups):
        make(yb, groups - 1)
        use(ya, total, first, groups - 2)
        use(yb, total, first, groups - 1)

    head(from_slices, acc, upper, HALF // 4)
    tail(from_slices, acc, upper, HALF // 4)
    for k in range(NT):
        pb[k] = acc[k * QROWS:(k + 1) * QROWS].astype(BF16)
    a2a = [remote(pb.at[t], ra.at[y], r, t) for t in (yp, ym, yo)]
    ex = [remote(pb.at[y], rb.at[y], outer, y)]
    ra[y] = pb[y]

    mm[0, yo] = dot_t(pk[0], own_sw[yo])
    mix_own(0)
    head(from_rows(tt), dfull, 0, MU // 4)

    tail(from_rows(tt), dfull, 0, MU // 4)

    for copy, t in zip(a2a, (ym, yp, yo)):
        copy.wait_recv()
        ex.append(remote(ra.at[t], rb.at[t], outer, y))
    dfull[...] = 0.5 * (dfull[...] + dfull[...].T)
    db[...] = dfull[...].astype(BF16)
    dx = [remote(db, dn.at[0], inner, y), remote(db, dn.at[1], outer, y)]

    in_o[1].wait_recv()
    moments(yo, 1)
    mix_own(1)
    tin_copy.wait_recv()

    head(from_rows(tin), acc, lower, HALF // 4)
    tail(from_rows(tin), acc, lower, HALF // 4)
    pin[...] = acc[...].astype(BF16)
    ex_in = remote(pin, rin, inner, y)
    turned[0] = acc[...].T
    turned[1] = ra[...].reshape(ROWS, ROWS).astype(F32).T

    d_high, d_low = split(dfull[...])
    diag = dfull[...] + dot(d_high, d_high) + dot(d_high, d_low) + dot(d_low, d_high)
    for side in (1, 0):
        dx[side].wait_recv()
        if side == 1:
            for copy in ex:
                copy.wait_recv()
            came = rb[...].reshape(ROWS, ROWS)
        else:
            ex_in.wait_recv()
            came = rin[...]
        place = (2 - 2 * core) if side == 0 else 2 * core
        keep = pat[0, place].astype(F32)
        block = keep * (came.astype(F32) + turned[side])
        high, low = split(block)
        diag = diag + dot_t(high, high) + dot_t(high, low) + dot_t(low, high)
        result = (block + dot(d_high, high) + dot(d_high, low) + dot(d_low, high)
                  + dot(high, dn[side]) + dot(low, dn[side]))
        out_ref[0, :, pl.ds(pl.multiple_of(place * ROWS, ROWS), ROWS)] = keep * result
    out_ref[0, :, ROWS:2 * ROWS] = pat[0, 1].astype(F32) * diag

    for copy in started:
        copy.wait_send()


COPIES = 48


def local(n_reg, tensor, g_occ, g_virt, offsets, pattern):
    anyspace = pl.BlockSpec(memory_space=pl.ANY)
    vmem = pl.BlockSpec(memory_space=pltpu.VMEM)
    return pl.pallas_call(
        functools.partial(kernel, n_reg),
        out_shape=pltpu.VMEM((1, ROWS, 3 * ROWS), F32),
        in_specs=[anyspace, anyspace, anyspace, vmem, pl.BlockSpec(memory_space=pltpu.SMEM)],
        out_specs=vmem,
        scratch_shapes=[
            pltpu.VMEM((ROWS, 2 * MU, NU), BF16),
            pltpu.VMEM((ROWS, MU * 256), BF16),
            pltpu.VMEM((ROWS, HALF * 256), BF16),
            pltpu.VMEM((QROWS, 2 * HALF, NU), BF16),
            pltpu.VMEM((HALF * QROWS, 256), BF16),
            pltpu.VMEM((NT, 5, 2, NU, LAM), BF16),
            pltpu.VMEM((1, 2), jnp.int32),
            pltpu.VMEM((1, 2), jnp.int32),
            pltpu.VMEM((3, 256, 256), BF16),
            pltpu.VMEM((NT, 256, 256), BF16),
            pltpu.VMEM((3, NT, 256, 256), F32),
            pltpu.VMEM((NT, 256, 256), F32),
            pltpu.VMEM((256, NT * 256), BF16),
            pltpu.VMEM((256, 256), BF16),
            pltpu.VMEM((256, 256), F32),
            pltpu.VMEM((NT, QROWS, 256), BF16),
            pltpu.VMEM((NT, QROWS, 256), BF16),
            pltpu.VMEM((NT, QROWS, 256), BF16),
            pltpu.VMEM((ROWS, ROWS), BF16),
            pltpu.VMEM((ROWS, ROWS), BF16),
            pltpu.VMEM((2, ROWS, ROWS), F32),
            pltpu.VMEM((256, 256), BF16),
            pltpu.VMEM((2, 256, 256), BF16),
            pltpu.VMEM((256, 256), F32),
            pltpu.VMEM((256, 1024), BF16),
            pltpu.VMEM((256, 1024), BF16),
            pltpu.SemaphoreType.DMA((6,)),
            pltpu.SemaphoreType.DMA((COPIES,)),
            pltpu.SemaphoreType.DMA((COPIES,)),
        ],
        compiler_params=pltpu.CompilerParams(collective_id=0, has_side_effects=True),
        name="screen",
    )(tensor.reshape(ROWS, 2 * MU, NU), g_occ, g_virt, offsets, pattern)


def solution(mesh):
    return jax.shard_map(
        functools.partial(local, mesh.shape["region"]),
        mesh=mesh,
        in_specs=(
            P("region", None, None, None),
            P("tm", "region", None),
            P("tm", "region", None),
            P("region", None),
            P("region", None),
        ),
        out_specs=P("tm", "region", None),
        check_vma=False,
    )
```
